32 devices in a mesh: exp: 16 (over z, y, core), strip: 2 (over x).
Axes of the slice: x: 2, y: 2, z: 4, core: 2. Of those that a mesh axis runs over, the one named last changes fastest.
Arguments:
- model: float32 [512, 2048], P('strip', 'exp'), may hold values from -6 to 6
- images: bfloat16 [16, 512, 2048], P('exp', 'strip'), may hold values from -6 to 6
- footprint: int32 [16, 4], replicated, may hold values from 0 to 2048, as said below
- psf_index: int32 [16], replicated, may hold values from 0 to 7, as said below
- exposure_weight: float32 [16], replicated, may hold values from 0.05 to 0.5
- psf_rows: bfloat16 [8, 4, 25], replicated, may hold values from -1.1953125 to 1.1953125
- psf_cols: bfloat16 [8, 4, 25], replicated, may hold values from -1.1953125 to 1.1953125
Outputs:
- new_model: float32 [512, 2048], P('strip', 'exp')
The draws below stay inside these ranges and needn't reach their ends.
Inputs may be any that keep to these rules, and one draw needn't show every extreme that they name: `footprint`: each exposure spans 128 or more rows and 512 or more columns; one exposure spans the whole sky. `psf_index`: every PSF model is used by the same number of exposures.
All inputs are finite; a program needn't handle non-finite values.
Results may differ from the reference program's by a relative error of at most 0.005.
Values may be sent and summed in bfloat16 or wider, within the bound.
A program may use at most 128 MiB of HBM per device.

```python
import math
import jax
import jax.numpy as jnp
from jax import lax

RANK = 4
TAPS = 25
BASIS = 8
EXPOSURES = 16
NR = 512
NC = 2048


def draw_footprint(key, part):
    subkeys = jax.random.split(key, 5)
    row_length = jax.random.randint(subkeys[0], (EXPOSURES,), NR // 4, NR + 1)
    row_start = jax.random.randint(subkeys[1], (EXPOSURES,), 0, NR - row_length + 1)
    col_length = jax.random.randint(subkeys[2], (EXPOSURES,), NC // 4, NC + 1)
    col_start = jax.random.randint(subkeys[3], (EXPOSURES,), 0, NC - col_length + 1)
    full_pick = jax.random.randint(subkeys[4], (), 0, EXPOSURES)
    chosen = jnp.arange(EXPOSURES) == full_pick
    row_start = jnp.where(chosen, 0, row_start)
    row_length = jnp.where(chosen, NR, row_length)
    col_start = jnp.where(chosen, 0, col_start)
    col_length = jnp.where(chosen, NC, col_length)
    return jnp.stack([row_start, row_start + row_length, col_start, col_start + col_length], axis=1).astype(jnp.int32)


def draw_psf_index(key, part):
    return (jax.random.permutation(key, EXPOSURES) % BASIS).astype(jnp.int32)


def level_of(rng, shape, shards, low, high):
    def one(dim, parts):
        steps = jax.random.uniform(jax.random.fold_in(jax.random.fold_in(rng, 6), dim), (parts,), jnp.float32, low / len(shards), high / len(shards))
        return jnp.repeat(jnp.exp(steps), shape[dim] // parts).reshape((-1,) + (1,) * (len(shape) - dim - 1))

    loudness = one(*shards[0])
    for cut in shards[1:]:
        loudness = loudness * one(*cut)
    return loudness


def gaussian(rng, shape, width, bound, cuts=(), held_as=jnp.bfloat16):
    array = width * jax.random.normal(rng, shape, jnp.float32)
    if cuts:
        array = array * level_of(rng, shape, cuts, -0.22, 0.18)
    return jnp.clip(array, -bound, bound).astype(held_as)


def setup_inputs(seed: int = 0) -> dict:
    streams_of = jax.random.split(jax.random.key(seed), 8)
    model = gaussian(streams_of[0], (NR, NC), 1.0, 6.0, ((0, 2), (1, 16)), jnp.float32)
    images = gaussian(streams_of[1], (EXPOSURES, NR, NC), 1.0, 6.0, ((0, 16), (1, 2)))
    footprint = draw_footprint(jax.random.fold_in(streams_of[7], 71), 0)
    psf_index = draw_psf_index(jax.random.fold_in(streams_of[7], 71), 0)
    exposure_weight = jnp.clip(jnp.exp(jax.random.uniform(streams_of[4], (EXPOSURES,), jnp.float32, math.log(0.05), math.log(0.5))), 0.05, 0.5)
    psf_rows = gaussian(streams_of[5], (BASIS, RANK, TAPS), 0.2, 1.1953125)
    psf_cols = gaussian(streams_of[6], (BASIS, RANK, TAPS), 0.2, 1.1953125)
    return {"model": model, "images": images, "footprint": footprint, "psf_index": psf_index, "exposure_weight": exposure_weight, "psf_rows": psf_rows, "psf_cols": psf_cols}


step_size = 0.25


def convolve(source, kernel, pads):
    return lax.conv_general_dilated(source, kernel, (1, 1), pads, dimension_numbers=("NCHW", "OIHW", "NCHW"), precision=lax.Precision.HIGHEST)


def rounded(values):
    return lax.optimization_barrier(values.astype(jnp.bfloat16)).astype(jnp.float32)


def reference(model, images, footprint, psf_index, exposure_weight, psf_rows, psf_cols):
    half_taps = TAPS // 2
    model_half = rounded(model)[None, None]
    row_taps = psf_rows.astype(jnp.float32)[psf_index]
    col_taps = psf_cols.astype(jnp.float32)[psf_index]
    sky_rows = jnp.arange(NR, dtype=jnp.int32)[:, None]
    sky_cols = jnp.arange(NC, dtype=jnp.int32)[None, :]
    along_rows = ((half_taps, half_taps), (0, 0))
    along_cols = ((0, 0), (half_taps, half_taps))

    def exposure_step(running, members):
        exposure_image, bounds, row_factor, col_factor, weight = members
        row_pass = rounded(convolve(model_half, row_factor[:, None, :, None], along_rows))
        predicted = convolve(row_pass, col_factor[None, :, None, :], along_cols)[0, 0]
        inside = (sky_rows >= bounds[0]) & (sky_rows < bounds[1]) & (sky_cols >= bounds[2]) & (sky_cols < bounds[3])
        residual = rounded(jnp.where(inside, weight * (predicted - exposure_image.astype(jnp.float32)), 0.0))
        back_cols = rounded(convolve(residual[None, None], col_factor[:, None, None, ::-1], along_cols))
        spread = convolve(back_cols, row_factor[None, :, ::-1, None], along_rows)[0, 0]
        return running + spread, None

    scanned = lax.scan(exposure_step, jnp.zeros((NR, NC), jnp.float32), (images, footprint, row_taps, col_taps, exposure_weight))
    return model - step_size * scanned[0]
```

```python
import functools

import jax
import jax.numpy as jnp
from jax import lax
from jax.experimental import pallas as pl
from jax.experimental.pallas import tpu as pltpu
from jax.sharding import PartitionSpec as P

RANK = 4
TAPS = 25
HALF = TAPS // 2
RIM = 16
LANES = 128
step_size = 0.25
MESH = pl.DeviceIdType.MESH
VMEM = pl.BlockSpec(memory_space=pltpu.VMEM)
SMEM = pl.BlockSpec(memory_space=pltpu.SMEM)


def places(n):
    line = n // 4
    if line < 8:
        split = lambda i: (i // 4, (i // 2) % 2, i % 2)
        join = lambda l, p, c: l * 4 + p * 2 + c
    else:
        split = lambda i: ((i // 2) % line, i // (2 * line), i % 2)
        join = lambda l, p, c: p * (2 * line) + l * 2 + c
    return line, split, join


def greet(devices):
    barrier = pltpu.get_barrier_semaphore()
    for device in devices:
        pl.semaphore_signal(barrier, inc=1, device_id=device, device_id_type=MESH)
    pl.semaphore_wait(barrier, len(devices))


def gather_kernel(n, strips, model_ref, x_ref, halo_send, halo_recv, line_send, line_recv,
                  pair_send, pair_recv, core_send, core_recv):
    line, split, join = places(n)
    me = lax.axis_index("exp")
    strip = lax.axis_index("strip")
    l, p, c = split(me)
    rows = model_ref.shape[0]
    above = {"strip": (strip + strips - 1) % strips}
    below = {"strip": (strip + 1) % strips}
    peers = [{"exp": join((l + q) % line, p, c)} for q in range(line)]
    pair = {"exp": join(l, 1 - p, c)}
    core = {"exp": join(l, p, 1 - c)}

    def push(src, dst, send, recv, device):
        copy = pltpu.make_async_remote_copy(
            src_ref=src, dst_ref=dst, send_sem=send, recv_sem=recv, device_id=device,
            device_id_type=MESH,
        )
        copy.start()
        return copy

    x_ref[me, RIM : RIM + rows, :] = model_ref[...].astype(jnp.bfloat16)
    greet([above, below, pair, core] + peers[1:])
    halos = [
        push(x_ref.at[me, pl.ds(RIM, RIM)], x_ref.at[me, pl.ds(RIM + rows, RIM)],
             halo_send.at[0], halo_recv.at[0], above),
        push(x_ref.at[me, pl.ds(rows, RIM)], x_ref.at[me, pl.ds(0, RIM)],
             halo_send.at[1], halo_recv.at[1], below),
    ]
    for copy in halos:
        copy.wait()
    order = [0]
    for q in range(1, line // 2 + 1):
        order += [q, line - q] if q != line - q else [q]
    along = {}
    for q in reversed(order[1:]):
        along[q] = push(x_ref.at[me], x_ref.at[me], line_send.at[q], line_recv.at[q], peers[q])
    over, across = [], []
    for q in order:
        slot = join((l + line - q) % line, p, c)
        if q:
            along[q].wait_recv()
        over.append(
            push(x_ref.at[slot], x_ref.at[slot], pair_send.at[q], pair_recv.at[q], pair)
        )
        across.append(
            push(x_ref.at[slot], x_ref.at[slot], core_send.at[q], core_recv.at[q], core)
        )
    for place, q in enumerate(order):
        slot = join((l + line - q) % line, 1 - p, c)
        over[place].wait_recv()
        across.append(
            push(x_ref.at[slot], x_ref.at[slot], core_send.at[line + q], core_recv.at[line + q],
                 core)
        )
    for copy in across:
        copy.wait()
    for copy in over:
        copy.wait_send()
    for q in order[1:]:
        along[q].wait_send()


def gather(n, strips, model):
    line = n // 4
    rows = model.shape[0]
    dma = pltpu.SemaphoreType.DMA
    return pl.pallas_call(
        functools.partial(gather_kernel, n, strips),
        out_shape=jax.ShapeDtypeStruct((n, rows + 2 * RIM, LANES), jnp.bfloat16),
        in_specs=[VMEM],
        out_specs=VMEM,
        scratch_shapes=[dma((2,)), dma((2,)), dma((line,)), dma((line,)), dma((line,)),
                        dma((line,)), dma((2 * line,)), dma((2 * line,))],
        compiler_params=pltpu.CompilerParams(collective_id=0, has_side_effects=True),
    )(model)


def compute_kernel(n, strips, rows_part, footprint, psf_index, weights, psf_rows, psf_cols, image,
                   x_ref, g_ref, lift, drop, fore, back, rp, res):
    f32, bf16 = jnp.float32, jnp.bfloat16
    me = lax.axis_index("exp")
    strip = lax.axis_index("strip")
    rows = image.shape[0]
    wide = n * LANES
    chosen = psf_index[me]

    def taps_of(table):
        total = jnp.zeros((RANK, TAPS), f32)
        for b in range(table.shape[0]):
            total = total + jnp.where(chosen == b, table[b].astype(f32), 0.0)
        return total.astype(bf16)

    tap = lax.broadcasted_iota(jnp.int32, (TAPS, 384), 0)
    lane = lax.broadcasted_iota(jnp.int32, (TAPS, 384), 1)
    same = (tap == lane).astype(f32).astype(bf16)
    mirror = (tap + lane == TAPS - 1).astype(f32).astype(bf16)
    row_taps = jnp.dot(taps_of(psf_rows), same, preferred_element_type=f32)
    col_taps = taps_of(psf_cols)
    col_fore = jnp.dot(col_taps, mirror, preferred_element_type=f32)
    col_back = jnp.dot(col_taps, same, preferred_element_type=f32)

    def slanted(vector, width, shift):
        spread = jnp.broadcast_to(vector[:, :width], (LANES, width))
        return pltpu.roll(pltpu.roll(spread, 0, 1, stride=1, stride_axis=0), shift, 1)

    fore[...] = jnp.zeros_like(fore)
    back[...] = jnp.zeros_like(back)
    for k in range(RANK):
        band = slanted(row_taps[k : k + 1], 256, RIM - HALF)
        lift[k * LANES : (k + 1) * LANES, :] = band[:, : LANES + 2 * RIM].astype(bf16)
        drop[:, k * LANES : (k + 1) * LANES] = band.T[: LANES + 2 * RIM].astype(bf16)
        for ref, vectors in ((fore, col_fore), (back, col_back)):
            strip_band = slanted(vectors[k : k + 1], 384, LANES - HALF).astype(bf16)
            for o in range(2):
                for d in range(3):
                    ref[k, (o + d) * LANES : (o + d + 1) * LANES, o * LANES : (o + 1) * LANES] = (
                        strip_band[:, (2 - d) * LANES : (3 - d) * LANES]
                    )

    edge = jnp.zeros((rows, LANES), bf16)
    for k in range(RANK):
        rp[k, :, :LANES] = edge
        rp[k, :, wide + LANES :] = edge
    res[:, :LANES] = edge
    res[:, wide + LANES :] = edge

    top = jnp.where(strip > 0, 1.0, 0.0)
    bottom = jnp.where(strip < strips - 1, 1.0, 0.0)
    parts = rows // LANES
    window = LANES + 2 * RIM

    def row_step(b, carry):
        left = x_ref[2 * b]
        right = x_ref[2 * b + 1]
        cells = jnp.concatenate([left, right], axis=1)
        upper = (cells[:RIM].astype(f32) * top).astype(bf16)
        lower = (cells[rows + RIM :].astype(f32) * bottom).astype(bf16)
        cells = jnp.concatenate([upper, cells[RIM : rows + RIM], lower], axis=0)
        at = pl.ds(pl.multiple_of(256 * b + LANES, LANES), 256)
        for s in range(parts):
            out = jnp.dot(lift[...], cells[s * LANES : s * LANES + window],
                          preferred_element_type=f32).astype(bf16)
            for k in range(RANK):
                rp[k, s * LANES : (s + 1) * LANES, at] = out[k * LANES : (k + 1) * LANES]
        return carry

    lax.fori_loop(0, n // 2, row_step, 0)

    weight = weights[me]
    row_at = lax.broadcasted_iota(jnp.int32, (rows, 256), 0) + strip * rows
    col_at = lax.broadcasted_iota(jnp.int32, (rows, 256), 1)
    row_ok = (row_at >= footprint[me, 0]) & (row_at < footprint[me, 1])
    start, stop = footprint[me, 2], footprint[me, 3]

    def fore_step(b, carry):
        begin = pl.multiple_of(256 * b, 256)
        predicted = jnp.zeros((rows, 256), f32)
        for k in range(RANK):
            predicted = predicted + jnp.dot(rp[k, :, pl.ds(begin, 512)], fore[k],
                                            preferred_element_type=f32)
        inside = row_ok & (col_at >= start - 256 * b) & (col_at < stop - 256 * b)
        value = weight * (predicted - image[:, pl.ds(begin, 256)].astype(f32))
        res[:, pl.ds(pl.multiple_of(256 * b + LANES, LANES), 256)] = jnp.where(
            inside, value, 0.0
        ).astype(bf16)
        return carry

    lax.fori_loop(0, n // 2, fore_step, 0)

    def back_step(b, carry):
        cells = res[:, pl.ds(pl.multiple_of(256 * b, 256), 512)]
        spread = [
            jnp.dot(cells, back[k], preferred_element_type=f32).astype(bf16) for k in range(RANK)
        ]
        total = jnp.zeros((rows + 2 * RIM, 256), f32)
        pieces = []
        for s in range(parts):
            stack = jnp.concatenate([v[s * LANES : (s + 1) * LANES] for v in spread], axis=0)
            pieces.append(jnp.dot(drop[...], stack, preferred_element_type=f32))
        joined = [pieces[0][:LANES]]
        for s in range(1, parts):
            joined.append(pieces[s - 1][LANES:] + pieces[s][: 2 * RIM])
            joined.append(pieces[s][2 * RIM : LANES])
        joined.append(pieces[-1][LANES:])
        total = jnp.concatenate(joined, axis=0).astype(bf16)
        g_ref[2 * b] = total[:, :LANES]
        g_ref[2 * b + 1] = total[:, LANES:]
        return carry

    lax.fori_loop(0, n // 2, back_step, 0)


def compute(n, strips, footprint, psf_index, weights, psf_rows, psf_cols, image, x):
    rows = image.shape[0]
    bf16 = jnp.bfloat16
    window = LANES + 2 * RIM
    return pl.pallas_call(
        functools.partial(compute_kernel, n, strips, rows),
        out_shape=jax.ShapeDtypeStruct(x.shape, bf16),
        in_specs=[SMEM, SMEM, SMEM, VMEM, VMEM, VMEM, VMEM],
        out_specs=VMEM,
        scratch_shapes=[
            pltpu.VMEM((RANK * LANES, window), bf16),
            pltpu.VMEM((window, RANK * LANES), bf16),
            pltpu.VMEM((RANK, 4 * LANES, 2 * LANES), bf16),
            pltpu.VMEM((RANK, 4 * LANES, 2 * LANES), bf16),
            pltpu.VMEM((RANK, rows, (n + 2) * LANES), bf16),
            pltpu.VMEM((rows, (n + 2) * LANES), bf16),
        ],
    )(footprint, psf_index, weights, psf_rows, psf_cols, image, x)


def scatter_kernel(n, strips, g_ref, out_ref, got_core, got_pair, got_line, to_pair, to_line, rims,
                   got_rims, core_send, core_recv, pair_send, pair_recv, line_send, line_recv,
                   rim_send, rim_recv):
    f32, bf16 = jnp.float32, jnp.bfloat16
    line, split, join = places(n)
    me = lax.axis_index("exp")
    strip = lax.axis_index("strip")
    l, p, c = split(me)
    rows = out_ref.shape[0]
    above = {"strip": (strip + strips - 1) % strips}
    below = {"strip": (strip + 1) % strips}
    peers = [{"exp": join((l + q) % line, p, c)} for q in range(line)]
    pair = {"exp": join(l, 1 - p, c)}
    core = {"exp": join(l, p, 1 - c)}

    def push(src, dst, send, recv, device):
        copy = pltpu.make_async_remote_copy(
            src_ref=src, dst_ref=dst, send_sem=send, recv_sem=recv, device_id=device,
            device_id_type=MESH,
        )
        copy.start()
        return copy

    order = [0]
    for q in range(1, line // 2 + 1):
        order += [q, line - q] if q != line - q else [q]
    order = order[::-1]
    greet([above, below, pair, core] + peers[1:])
    swaps = {}
    for t, side in ((0, 1 - p), (1, p)):
        for q in order:
            at = t * line + q
            swaps[at] = push(g_ref.at[join((l + q) % line, side, 1 - c)], got_core.at[at],
                             core_send.at[at], core_recv.at[at], core)
    over = {}
    for q in order:
        swaps[q].wait_recv()
        to_pair[q] = (
            g_ref[join((l + q) % line, 1 - p, c)].astype(f32) + got_core[q].astype(f32)
        ).astype(bf16)
        over[q] = push(to_pair.at[q], got_pair.at[q], pair_send.at[q], pair_recv.at[q], pair)
    along = {}
    for q in order:
        swaps[line + q].wait_recv()
        over[q].wait_recv()
        part = (
            g_ref[join((l + q) % line, p, c)].astype(f32)
            + got_core[line + q].astype(f32)
            + got_pair[q].astype(f32)
        )
        if q:
            to_line[q] = part.astype(bf16)
            along[q] = push(to_line.at[q], got_line.at[q], line_send.at[q], line_recv.at[q],
                            peers[q])
        else:
            total = part
    for q in order[::-1][1:]:
        along[q].wait_recv()
        total = total + got_line[q].astype(f32)
    rims[0] = total[:RIM]
    rims[1] = total[rows + RIM :]
    out_ref[...] = total[RIM : rows + RIM]
    edges = [
        push(rims.at[0], got_rims.at[0], rim_send.at[0], rim_recv.at[0], above),
        push(rims.at[1], got_rims.at[1], rim_send.at[1], rim_recv.at[1], below),
    ]
    for copy in swaps.values():
        copy.wait_send()
    for copy in over.values():
        copy.wait_send()
    for copy in along.values():
        copy.wait_send()
    for copy in edges:
        copy.wait()
    has_below = jnp.where(strip < strips - 1, 1.0, 0.0)
    has_above = jnp.where(strip > 0, 1.0, 0.0)
    out_ref[rows - RIM :, :] = out_ref[rows - RIM :, :] + got_rims[0] * has_below
    out_ref[:RIM, :] = out_ref[:RIM, :] + got_rims[1] * has_above


def scatter(n, strips, g):
    line = n // 4
    high = g.shape[1]
    bf16 = jnp.bfloat16
    dma = pltpu.SemaphoreType.DMA
    return pl.pallas_call(
        functools.partial(scatter_kernel, n, strips),
        out_shape=jax.ShapeDtypeStruct((high - 2 * RIM, LANES), jnp.float32),
        in_specs=[VMEM],
        out_specs=VMEM,
        scratch_shapes=[
            pltpu.VMEM((2 * line, high, LANES), bf16),
            pltpu.VMEM((line, high, LANES), bf16),
            pltpu.VMEM((line, high, LANES), bf16),
            pltpu.VMEM((line, high, LANES), bf16),
            pltpu.VMEM((line, high, LANES), bf16),
            pltpu.VMEM((2, RIM, LANES), jnp.float32),
            pltpu.VMEM((2, RIM, LANES), jnp.float32),
            dma((2 * line,)), dma((2 * line,)), dma((line,)), dma((line,)), dma((line,)),
            dma((line,)), dma((2,)), dma((2,)),
        ],
        compiler_params=pltpu.CompilerParams(collective_id=1, has_side_effects=True),
    )(g)


def solution(mesh):
    n, strips = mesh.shape["exp"], mesh.shape["strip"]

    def local(model, images, footprint, psf_index, exposure_weight, psf_rows, psf_cols):
        x = gather(n, strips, model)
        g = compute(n, strips, footprint, psf_index, exposure_weight, psf_rows, psf_cols,
                    images[0], x)
        return model - step_size * scatter(n, strips, g)

    placed = (P("strip", "exp"), P("exp", "strip", None), P(), P(), P(), P(), P())
    return jax.shard_map(
        local, mesh=mesh, in_specs=placed, out_specs=P("strip", "exp"), check_vma=False
    )
```

```python
import functools

import jax
import jax.numpy as jnp
from jax import lax
from jax.experimental import pallas as pl
from jax.experimental.pallas import tpu as pltpu
from jax.sharding import PartitionSpec as P

RANK = 4
TAPS = 25
HALF = TAPS // 2
RIM = 16
LANES = 128
step_size = 0.25
MESH = pl.DeviceIdType.MESH
VMEM = pl.BlockSpec(memory_space=pltpu.VMEM)
SMEM = pl.BlockSpec(memory_space=pltpu.SMEM)


def places(n):
    line = n // 4
    if line < 8:
        split = lambda i: (i // 4, (i // 2) % 2, i % 2)
        join = lambda l, p, c: l * 4 + p * 2 + c
    else:
        split = lambda i: ((i // 2) % line, i // (2 * line), i % 2)
        join = lambda l, p, c: p * (2 * line) + l * 2 + c
    return line, split, join


def push(src, dst, send, recv, device):
    copy = pltpu.make_async_remote_copy(
        src_ref=src, dst_ref=dst, send_sem=send, recv_sem=recv, device_id=device,
        device_id_type=MESH,
    )
    copy.start()
    return copy


def greet(devices):
    barrier = pltpu.get_barrier_semaphore()
    for device in devices:
        pl.semaphore_signal(barrier, inc=1, device_id=device, device_id_type=MESH)
    pl.semaphore_wait(barrier, len(devices))


def step_kernel(n, strips, model_ref, footprint, psf_index, weights, psf_rows, psf_cols, image_ref,
                out_ref, image, x, edge, lift, drop, fore, back, pred, res, g, rim, got_rim,
                got_core, to_pair, got_pair, to_line, got_line, image_sem, line_sems, pair_sems,
                core_sems, edge_sems, swap_sems, over_sems, along_sems, rim_sems):
    f32, bf16 = jnp.float32, jnp.bfloat16
    line, split, join = places(n)
    me = lax.axis_index("exp")
    strip = lax.axis_index("strip")
    l, p, c = split(me)
    rows = model_ref.shape[0]
    wide = n * LANES
    parts = rows // LANES
    window = LANES + 2 * RIM
    above, below = (strip + strips - 1) % strips, (strip + 1) % strips
    peers = [{"exp": join((l + q) % line, p, c)} for q in range(line)]
    partner = join(l, p, 1 - c)
    pair = {"exp": join(l, 1 - p, c)}
    core = {"exp": partner}
    aboves = [{"strip": above, "exp": me}, {"strip": above, "exp": partner}]
    belows = [{"strip": below, "exp": me}, {"strip": below, "exp": partner}]

    order = [0]
    for q in range(1, line // 2 + 1):
        order += [q, line - q] if q != line - q else [q]

    fetch = pltpu.make_async_copy(image_ref, image, image_sem)
    fetch.start()
    x[me] = model_ref[...].astype(bf16)
    greet(aboves + belows + [pair, core] + peers[1:])
    along, over, across, edges = {}, {}, {}, {}

    def spread_slot(at, slot):
        across[at] = push(x.at[slot], x.at[slot], core_sems.at[0, at], core_sems.at[1, at], core)
        for cc in range(2):
            edges[at, cc, 0] = push(
                x.at[slot, pl.ds(rows - RIM, RIM)], edge.at[slot, 0],
                edge_sems.at[0, at, cc, 0], edge_sems.at[1, at, cc, 0], belows[cc],
            )
            edges[at, cc, 1] = push(
                x.at[slot, pl.ds(0, RIM)], edge.at[slot, 1],
                edge_sems.at[0, at, cc, 1], edge_sems.at[1, at, cc, 1], aboves[cc],
            )

    def forward_line(q):
        slot = join((l + line - q) % line, p, c)
        if q:
            along[q].wait_recv()
        over[q] = push(x.at[slot], x.at[slot], pair_sems.at[0, q], pair_sems.at[1, q], pair)
        spread_slot(q, slot)

    def forward_pair(q):
        over[q].wait_recv()
        spread_slot(line + q, join((l + line - q) % line, 1 - p, c))

    for q in order[:0:-1]:
        along[q] = push(x.at[me], x.at[me], line_sems.at[0, q], line_sems.at[1, q], peers[q])
    forward_line(0)

    chosen = psf_index[me]

    def taps_of(table):
        total = jnp.zeros((RANK, TAPS), f32)
        for b in range(table.shape[0]):
            total = total + jnp.where(chosen == b, table[b].astype(f32), 0.0)
        return total.astype(bf16)

    tap = lax.broadcasted_iota(jnp.int32, (TAPS, 384), 0)
    lane = lax.broadcasted_iota(jnp.int32, (TAPS, 384), 1)
    same = (tap == lane).astype(f32).astype(bf16)
    mirror = (tap + lane == TAPS - 1).astype(f32).astype(bf16)
    row_taps = jnp.dot(taps_of(psf_rows), same, preferred_element_type=f32)
    col_taps = taps_of(psf_cols)
    col_fore = jnp.dot(col_taps, mirror, preferred_element_type=f32)
    col_back = jnp.dot(col_taps, same, preferred_element_type=f32)

    def slanted(vector, width, shift):
        spread = jnp.broadcast_to(vector[:, :width], (LANES, width))
        return pltpu.roll(pltpu.roll(spread, 0, 1, stride=1, stride_axis=0), shift, 1)

    none = jnp.zeros((LANES, LANES), bf16)
    for k in range(RANK):
        band = slanted(row_taps[k : k + 1], 256, RIM - HALF)
        lift[k * LANES : (k + 1) * LANES, :] = band[:, :window].astype(bf16)
        drop[:, k * LANES : (k + 1) * LANES] = band.T[:window].astype(bf16)
        band = slanted(col_fore[k : k + 1], 384, LANES - HALF).astype(bf16)
        fore[2 * k * LANES : (2 * k + 1) * LANES, :] = jnp.concatenate([band, none], axis=1)
        fore[(2 * k + 1) * LANES : (2 * k + 2) * LANES, :] = jnp.concatenate([none, band], axis=1)
        band = slanted(col_back[k : k + 1], 384, LANES - HALF).astype(bf16)
        for w in range(4):
            for o in range(2):
                d = w - o
                piece = band[:, (2 - d) * LANES : (3 - d) * LANES] if 0 <= d <= 2 else none
                at = (2 * k + o) * LANES
                back[w * LANES : (w + 1) * LANES, at : at + LANES] = piece
    pred[...] = jnp.zeros_like(pred)
    res[:, :LANES] = jnp.zeros((rows, LANES), bf16)
    res[:, wide + LANES :] = jnp.zeros((rows, LANES), bf16)

    top = jnp.where(strip > 0, 1.0, 0.0)
    bottom = jnp.where(strip < strips - 1, 1.0, 0.0)

    def fore_step(group):
        def step(side, carry):
            left = join(group, side, 0)
            right = left + 1
            upper = jnp.concatenate([edge[left, 0], edge[right, 0]], axis=1)
            lower = jnp.concatenate([edge[left, 1], edge[right, 1]], axis=1)
            upper = (upper.astype(f32) * top).astype(bf16)
            lower = (lower.astype(f32) * bottom).astype(bf16)
            middle = jnp.concatenate([x[left], x[right]], axis=1)
            cells = jnp.concatenate([upper, middle, lower], axis=0)
            passes = []
            for s in range(parts):
                out = jnp.dot(lift[...], cells[s * LANES : s * LANES + window],
                              preferred_element_type=f32).astype(bf16)
                passes.append(jnp.concatenate(
                    [out[k * LANES : (k + 1) * LANES] for k in range(RANK)], axis=1))
            stack = jnp.concatenate(passes, axis=0)
            at = pl.ds(pl.multiple_of(left * LANES, 2 * LANES), 4 * LANES)
            pred[:, at] = pred[:, at] + jnp.dot(stack, fore[...], preferred_element_type=f32)
            return carry

        lax.fori_loop(0, 2, step, 0)

    lines_done, pairs_done = 1, 0
    for i, q in enumerate(order):
        while lines_done < min(line, i + 3):
            forward_line(order[lines_done])
            lines_done += 1
        while pairs_done < min(line, i + 2 if i else 1):
            forward_pair(order[pairs_done])
            pairs_done += 1
        for at in (q, line + q):
            across[at].wait_recv()
            for cc in range(2):
                for side in range(2):
                    edges[at, cc, side].wait_recv()
        fore_step((l + line - q) % line)

    fetch.wait()
    weight = weights[me]
    first_row, last_row = footprint[0, me], footprint[1, me]
    first_col, last_col = footprint[2, me], footprint[3, me]
    row_at = lax.broadcasted_iota(jnp.int32, (rows, 256), 0) + strip * rows
    col_at = lax.broadcasted_iota(jnp.int32, (rows, 256), 1)
    row_ok = (row_at >= first_row) & (row_at < last_row)

    def residual_step(b, carry):
        begin = pl.multiple_of(256 * b, 256)
        inner = pl.ds(pl.multiple_of(256 * b + LANES, LANES), 256)
        inside = row_ok & (col_at >= first_col - begin) & (col_at < last_col - begin)
        value = weight * (pred[:, inner] - image[:, pl.ds(begin, 256)].astype(f32))
        res[:, inner] = jnp.where(inside, value, 0.0).astype(bf16)
        return carry

    lax.fori_loop(0, n // 2, residual_step, 0)

    def back_step(group):
        def step(side, carry):
            left = join(group, side, 0)
            cells = res[:, pl.ds(pl.multiple_of(left * LANES, 2 * LANES), 4 * LANES)]
            spread = jnp.dot(cells, back[...], preferred_element_type=f32).astype(bf16)
            pieces = []
            for s in range(parts):
                part = spread[s * LANES : (s + 1) * LANES]
                stack = jnp.concatenate(
                    [part[:, k * 256 : (k + 1) * 256] for k in range(RANK)], axis=0)
                pieces.append(jnp.dot(drop[...], stack, preferred_element_type=f32))
            joined = [pieces[0][RIM:LANES]]
            for s in range(1, parts):
                joined.append(pieces[s - 1][LANES:] + pieces[s][: 2 * RIM])
                joined.append(pieces[s][2 * RIM : LANES])
            joined.append(pieces[-1][LANES : LANES + RIM])
            total = jnp.concatenate(joined, axis=0).astype(bf16)
            first, last = pieces[0][:RIM].astype(bf16), pieces[-1][LANES + RIM :].astype(bf16)
            for o in range(2):
                cols = slice(o * LANES, (o + 1) * LANES)
                g[left + o] = total[:, cols]
                rim[left + o, 0] = first[:, cols]
                rim[left + o, 1] = last[:, cols]
            return carry

        lax.fori_loop(0, 2, step, 0)

    swaps, rims, onward, home = {}, {}, {}, {}

    def send_group(q):
        group = (l + q) % line
        back_step(group)
        for t, side in ((0, 1 - p), (1, p)):
            at = t * line + q
            swaps[at] = push(g.at[join(group, side, 1 - c)], got_core.at[at],
                             swap_sems.at[0, at], swap_sems.at[1, at], core)
            for cc, whose in ((0, c), (1, 1 - c)):
                slot = join(group, side, whose)
                rims[at, cc, 0] = push(
                    rim.at[slot, 0], got_rim.at[at, cc, 0],
                    rim_sems.at[0, at, cc, 0], rim_sems.at[1, at, cc, 0], aboves[cc])
                rims[at, cc, 1] = push(
                    rim.at[slot, 1], got_rim.at[at, cc, 1],
                    rim_sems.at[0, at, cc, 1], rim_sems.at[1, at, cc, 1], belows[cc])

    def chip_sum(at, slot):
        swaps[at].wait_recv()
        for cc in range(2):
            for side in range(2):
                rims[at, cc, side].wait_recv()
        total = g[slot].astype(f32) + got_core[at].astype(f32)
        low = (got_rim[at, 0, 0].astype(f32) + got_rim[at, 1, 0].astype(f32)) * bottom
        high = (got_rim[at, 0, 1].astype(f32) + got_rim[at, 1, 1].astype(f32)) * top
        return jnp.concatenate(
            [total[:RIM] + high, total[RIM : rows - RIM], total[rows - RIM :] + low], axis=0)

    def send_pair(q):
        to_pair[q] = chip_sum(q, join((l + q) % line, 1 - p, c)).astype(bf16)
        onward[q] = push(to_pair.at[q], got_pair.at[q], over_sems.at[0, q], over_sems.at[1, q],
                         pair)

    def send_line(q):
        total = chip_sum(line + q, join((l + q) % line, p, c))
        onward[q].wait_recv()
        total = total + got_pair[q].astype(f32)
        if q:
            to_line[q] = total.astype(bf16)
            home[q] = push(to_line.at[q], got_line.at[q], along_sems.at[0, q],
                           along_sems.at[1, q], peers[q])
        return total

    total = None
    for i in range(line + 2):
        if i < line:
            send_group(order[line - 1 - i])
        if 1 <= i < line + 1:
            send_pair(order[line - i])
        if i >= 2:
            total = send_line(order[line + 1 - i])
    for q in order[:0:-1]:
        home[q].wait_recv()
        total = total + got_line[q].astype(f32)
    out_ref[...] = total
    for group in (along, over, across, edges, swaps, rims, onward, home):
        for copy in group.values():
            copy.wait_send()


def solution(mesh):
    n, strips = mesh.shape["exp"], mesh.shape["strip"]
    line = n // 4
    f32, bf16 = jnp.float32, jnp.bfloat16
    dma = pltpu.SemaphoreType.DMA
    window = LANES + 2 * RIM

    def local(model, images, footprint, psf_index, exposure_weight, psf_rows, psf_cols):
        rows = model.shape[0]
        blocks = lambda count: pltpu.VMEM((count, rows, LANES), bf16)
        gradient = pl.pallas_call(
            functools.partial(step_kernel, n, strips),
            out_shape=jax.ShapeDtypeStruct(model.shape, f32),
            in_specs=[VMEM, SMEM, SMEM, SMEM, VMEM, VMEM, pl.BlockSpec(memory_space=pl.ANY)],
            out_specs=VMEM,
            scratch_shapes=[
                pltpu.VMEM((rows, n * LANES), bf16),
                blocks(n),
                pltpu.VMEM((n, 2, RIM, LANES), bf16),
                pltpu.VMEM((RANK * LANES, window), bf16),
                pltpu.VMEM((window, RANK * LANES), bf16),
                pltpu.VMEM((RANK * 2 * LANES, 4 * LANES), bf16),
                pltpu.VMEM((4 * LANES, RANK * 2 * LANES), bf16),
                pltpu.VMEM((rows, (n + 2) * LANES), f32),
                pltpu.VMEM((rows, (n + 2) * LANES), bf16),
                blocks(n),
                pltpu.VMEM((n, 2, RIM, LANES), bf16),
                pltpu.VMEM((2 * line, 2, 2, RIM, LANES), bf16),
                blocks(2 * line), blocks(line), blocks(line), blocks(line), blocks(line),
                dma, dma((2, line)), dma((2, line)), dma((2, 2 * line)),
                dma((2, 2 * line, 2, 2)), dma((2, 2 * line)), dma((2, line)), dma((2, line)),
                dma((2, 2 * line, 2, 2)),
            ],
            compiler_params=pltpu.CompilerParams(collective_id=0, has_side_effects=True),
        )(model, footprint.T, psf_index, exposure_weight, psf_rows, psf_cols, images[0])
        return model - step_size * gradient

    placed = (P("strip", "exp"), P("exp", "strip", None), P(), P(), P(), P(), P())
    return jax.shard_map(
        local, mesh=mesh, in_specs=placed, out_specs=P("strip", "exp"), check_vma=False
    )
```

```python
import functools

import jax
import jax.numpy as jnp
from jax import lax
from jax.experimental import pallas as pl
from jax.experimental.pallas import tpu as pltpu
from jax.sharding import PartitionSpec as P

RANK = 4
TAPS = 25
HALF = TAPS // 2
RIM = 16
LANES = 128
step_size = 0.25
MESH = pl.DeviceIdType.MESH
VMEM = pl.BlockSpec(memory_space=pltpu.VMEM)
SMEM = pl.BlockSpec(memory_space=pltpu.SMEM)


def places(n):
    line = n // 4
    if line < 8:
        split = lambda i: (i // 4, (i // 2) % 2, i % 2)
        join = lambda l, p, c: l * 4 + p * 2 + c
    else:
        split = lambda i: ((i // 2) % line, i // (2 * line), i % 2)
        join = lambda l, p, c: p * (2 * line) + l * 2 + c
    return line, split, join


def push(src, dst, send, recv, device):
    copy = pltpu.make_async_remote_copy(
        src_ref=src, dst_ref=dst, send_sem=send, recv_sem=recv, device_id=device,
        device_id_type=MESH,
    )
    copy.start()
    return copy


def greet(devices):
    barrier = pltpu.get_barrier_semaphore()
    for device in devices:
        pl.semaphore_signal(barrier, inc=1, device_id=device, device_id_type=MESH)
    pl.semaphore_wait(barrier, len(devices))


def step_kernel(n, strips, model_ref, footprint, psf_index, weights, psf_rows, psf_cols, image_ref,
                out_ref, image, x, edge, lift, drop, fore, back, pred, res, g, rim, got_rim,
                got_core, to_pair, got_pair, to_line, got_line, image_sem, line_sems, pair_sems,
                core_sems, halo_sems, rim_line_sems, rim_pair_sems,
                rim_core_sems, swap_sems, over_sems, along_sems, rim_sems):
    f32, bf16 = jnp.float32, jnp.bfloat16
    line, split, join = places(n)
    me = lax.axis_index("exp")
    strip = lax.axis_index("strip")
    l, p, c = split(me)
    rows = model_ref.shape[0]
    wide = n * LANES
    parts = rows // LANES
    window = LANES + 2 * RIM
    above, below = (strip + strips - 1) % strips, (strip + 1) % strips
    peers = [{"exp": join((l + q) % line, p, c)} for q in range(line)]
    partner = join(l, p, 1 - c)
    pair = {"exp": join(l, 1 - p, c)}
    core = {"exp": partner}
    aboves = [{"strip": above, "exp": me}, {"strip": above, "exp": partner}]
    belows = [{"strip": below, "exp": me}, {"strip": below, "exp": partner}]

    order = [0]
    for q in range(1, line // 2 + 1):
        order += [q, line - q] if q != line - q else [q]

    fetch = pltpu.make_async_copy(image_ref, image, image_sem)
    fetch.start()
    x[me] = model_ref[...].astype(bf16)
    greet(aboves + belows + [pair, core] + peers[1:])
    along, over, across, edges = {}, {}, {}, {}

    def send_core(at, slot):
        across[at] = push(x.at[slot], x.at[slot], core_sems.at[0, at], core_sems.at[1, at], core)

    def send_core_edge(at, slot):
        edges["core", at] = push(edge.at[slot], edge.at[slot], rim_core_sems.at[0, at],
                                 rim_core_sems.at[1, at], core)

    def send_over(q, slot):
        over[q] = push(x.at[slot], x.at[slot], pair_sems.at[0, q], pair_sems.at[1, q], pair)

    def send_over_edge(q, slot):
        edges["pair", q] = push(edge.at[slot], edge.at[slot], rim_pair_sems.at[0, q],
                                rim_pair_sems.at[1, q], pair)

    def forward_line(q):
        slot = join((l + line - q) % line, p, c)
        along[q].wait_recv()
        send_over(q, slot)
        send_core(q, slot)
        edges["line", q].wait_recv()
        send_over_edge(q, slot)
        send_core_edge(q, slot)

    def forward_pair(q):
        slot = join((l + line - q) % line, 1 - p, c)
        over[q].wait_recv()
        send_core(line + q, slot)
        edges["pair", q].wait_recv()
        send_core_edge(line + q, slot)

    halos = [
        push(x.at[me, pl.ds(rows - RIM, RIM)], edge.at[me, 0], halo_sems.at[0, 0],
             halo_sems.at[1, 0], {"strip": below}),
        push(x.at[me, pl.ds(0, RIM)], edge.at[me, 1], halo_sems.at[0, 1], halo_sems.at[1, 1],
             {"strip": above}),
    ]
    for q in order[1:]:
        along[q] = push(x.at[me], x.at[me], line_sems.at[0, q], line_sems.at[1, q], peers[q])
    send_over(0, me)
    send_core(0, me)

    chosen = psf_index[me]

    def taps_of(table):
        total = jnp.zeros((RANK, TAPS), f32)
        for b in range(table.shape[0]):
            total = total + jnp.where(chosen == b, table[b].astype(f32), 0.0)
        return total.astype(bf16)

    tap = lax.broadcasted_iota(jnp.int32, (TAPS, 384), 0)
    lane = lax.broadcasted_iota(jnp.int32, (TAPS, 384), 1)
    same = (tap == lane).astype(f32).astype(bf16)
    mirror = (tap + lane == TAPS - 1).astype(f32).astype(bf16)
    row_taps = jnp.dot(taps_of(psf_rows), same, preferred_element_type=f32)
    col_taps = taps_of(psf_cols)
    col_fore = jnp.dot(col_taps, mirror, preferred_element_type=f32)
    col_back = jnp.dot(col_taps, same, preferred_element_type=f32)

    def slanted(vector, width, shift):
        spread = jnp.broadcast_to(vector[:, :width], (LANES, width))
        return pltpu.roll(pltpu.roll(spread, 0, 1, stride=1, stride_axis=0), shift, 1)

    none = jnp.zeros((LANES, LANES), bf16)
    for k in range(RANK):
        band = slanted(row_taps[k : k + 1], 256, RIM - HALF)
        lift[k * LANES : (k + 1) * LANES, :] = band[:, :window].astype(bf16)
        band = slanted(col_fore[k : k + 1], 384, LANES - HALF).astype(bf16)
        fore[2 * k * LANES : (2 * k + 1) * LANES, :] = jnp.concatenate([band, none], axis=1)
        fore[(2 * k + 1) * LANES : (2 * k + 2) * LANES, :] = jnp.concatenate([none, band], axis=1)

    for copy in halos:
        copy.wait()
    for q in order[1:]:
        edges["line", q] = push(edge.at[me], edge.at[me], rim_line_sems.at[0, q],
                                rim_line_sems.at[1, q], peers[q])
    send_over_edge(0, me)
    send_core_edge(0, me)

    for k in range(RANK):
        band = slanted(row_taps[k : k + 1], 256, RIM - HALF)
        drop[:, k * LANES : (k + 1) * LANES] = band.T[:window].astype(bf16)
        band = slanted(col_back[k : k + 1], 384, LANES - HALF).astype(bf16)
        for w in range(4):
            for o in range(2):
                d = w - o
                piece = band[:, (2 - d) * LANES : (3 - d) * LANES] if 0 <= d <= 2 else none
                at = (2 * k + o) * LANES
                back[w * LANES : (w + 1) * LANES, at : at + LANES] = piece
    pred[...] = jnp.zeros_like(pred)
    res[:, :LANES] = jnp.zeros((rows, LANES), bf16)
    res[:, wide + LANES :] = jnp.zeros((rows, LANES), bf16)

    top = jnp.where(strip > 0, 1.0, 0.0)
    bottom = jnp.where(strip < strips - 1, 1.0, 0.0)

    def fore_step(at, group, side):
        across[at].wait_recv()
        edges["core", at].wait_recv()
        left = join(group, side, 0)
        right = left + 1
        upper = jnp.concatenate([edge[left, 0], edge[right, 0]], axis=1)
        lower = jnp.concatenate([edge[left, 1], edge[right, 1]], axis=1)
        upper = (upper.astype(f32) * top).astype(bf16)
        lower = (lower.astype(f32) * bottom).astype(bf16)
        middle = jnp.concatenate([x[left], x[right]], axis=1)
        cells = jnp.concatenate([upper, middle, lower], axis=0)
        passes = []
        for s in range(parts):
            out = jnp.dot(lift[...], cells[s * LANES : s * LANES + window],
                          preferred_element_type=f32).astype(bf16)
            passes.append(jnp.concatenate(
                [out[k * LANES : (k + 1) * LANES] for k in range(RANK)], axis=1))
        stack = jnp.concatenate(passes, axis=0)
        at = pl.ds(pl.multiple_of(left * LANES, 2 * LANES), 4 * LANES)
        pred[:, at] = pred[:, at] + jnp.dot(stack, fore[...], preferred_element_type=f32)

    def near_step(q):
        fore_step(q, (l + line - q) % line, p)

    def far_step(q):
        fore_step(line + q, (l + line - q) % line, 1 - p)

    near_step(0)
    forward_pair(0)
    for q in order[1:3]:
        forward_line(q)
    far_step(0)
    for i in range(1, line):
        near_step(order[i])
        forward_pair(order[i])
        if i + 2 < line:
            forward_line(order[i + 2])
        if i >= 2:
            far_step(order[i - 1])
    far_step(order[-1])

    fetch.wait()
    weight = weights[me]
    first_row, last_row = footprint[0, me], footprint[1, me]
    first_col, last_col = footprint[2, me], footprint[3, me]
    row_at = lax.broadcasted_iota(jnp.int32, (rows, 256), 0) + strip * rows
    col_at = lax.broadcasted_iota(jnp.int32, (rows, 256), 1)
    row_ok = (row_at >= first_row) & (row_at < last_row)

    def residual_step(b, carry):
        begin = pl.multiple_of(256 * b, 256)
        inner = pl.ds(pl.multiple_of(256 * b + LANES, LANES), 256)
        inside = row_ok & (col_at >= first_col - begin) & (col_at < last_col - begin)
        value = weight * (pred[:, inner] - image[:, pl.ds(begin, 256)].astype(f32))
        res[:, inner] = jnp.where(inside, value, 0.0).astype(bf16)
        return carry

    lax.fori_loop(0, n // 2, residual_step, 0)

    def back_step(group, side):
        left = join(group, side, 0)
        cells = res[:, pl.ds(pl.multiple_of(left * LANES, 2 * LANES), 4 * LANES)]
        spread = jnp.dot(cells, back[...], preferred_element_type=f32).astype(bf16)
        pieces = []
        for s in range(parts):
            part = spread[s * LANES : (s + 1) * LANES]
            stack = jnp.concatenate(
                [part[:, k * 256 : (k + 1) * 256] for k in range(RANK)], axis=0)
            pieces.append(jnp.dot(drop[...], stack, preferred_element_type=f32))
        joined = [pieces[0][RIM:LANES]]
        for s in range(1, parts):
            joined.append(pieces[s - 1][LANES:] + pieces[s][: 2 * RIM])
            joined.append(pieces[s][2 * RIM : LANES])
        joined.append(pieces[-1][LANES : LANES + RIM])
        total = jnp.concatenate(joined, axis=0).astype(bf16)
        first, last = pieces[0][:RIM].astype(bf16), pieces[-1][LANES + RIM :].astype(bf16)
        for o in range(2):
            cols = slice(o * LANES, (o + 1) * LANES)
            g[left + o] = total[:, cols]
            rim[left + o, 0] = first[:, cols]
            rim[left + o, 1] = last[:, cols]

    swaps, rims, onward, home = {}, {}, {}, {}

    def send_group(q):
        group = (l + q) % line
        for t, side in ((0, 1 - p), (1, p)):
            at = t * line + q
            back_step(group, side)
            swaps[at] = push(g.at[join(group, side, 1 - c)], got_core.at[at],
                             swap_sems.at[0, at], swap_sems.at[1, at], core)
            for cc, whose in ((0, c), (1, 1 - c)):
                slot = join(group, side, whose)
                rims[at, cc, 0] = push(
                    rim.at[slot, 0], got_rim.at[at, cc, 0],
                    rim_sems.at[0, at, cc, 0], rim_sems.at[1, at, cc, 0], aboves[cc])
                rims[at, cc, 1] = push(
                    rim.at[slot, 1], got_rim.at[at, cc, 1],
                    rim_sems.at[0, at, cc, 1], rim_sems.at[1, at, cc, 1], belows[cc])

    def chip_sum(at, slot):
        swaps[at].wait_recv()
        for cc in range(2):
            for side in range(2):
                rims[at, cc, side].wait_recv()
        total = g[slot].astype(f32) + got_core[at].astype(f32)
        low = (got_rim[at, 0, 0].astype(f32) + got_rim[at, 1, 0].astype(f32)) * bottom
        high = (got_rim[at, 0, 1].astype(f32) + got_rim[at, 1, 1].astype(f32)) * top
        return jnp.concatenate(
            [total[:RIM] + high, total[RIM : rows - RIM], total[rows - RIM :] + low], axis=0)

    def send_pair(q):
        to_pair[q] = chip_sum(q, join((l + q) % line, 1 - p, c)).astype(bf16)
        onward[q] = push(to_pair.at[q], got_pair.at[q], over_sems.at[0, q], over_sems.at[1, q],
                         pair)

    def send_line(q):
        total = chip_sum(line + q, join((l + q) % line, p, c))
        onward[q].wait_recv()
        total = total + got_pair[q].astype(f32)
        if q:
            to_line[q] = total.astype(bf16)
            home[q] = push(to_line.at[q], got_line.at[q], along_sems.at[0, q],
                           along_sems.at[1, q], peers[q])
        return total

    total = None
    for i in range(line + 2):
        if i < line:
            send_group(order[line - 1 - i])
        if 1 <= i < line + 1:
            send_pair(order[line - i])
        if i >= 2:
            total = send_line(order[line + 1 - i])
    for q in order[:0:-1]:
        home[q].wait_recv()
        total = total + got_line[q].astype(f32)
    out_ref[...] = total
    for group in (along, over, across, edges, swaps, rims, onward, home):
        for copy in group.values():
            copy.wait_send()


def solution(mesh):
    n, strips = mesh.shape["exp"], mesh.shape["strip"]
    line = n // 4
    f32, bf16 = jnp.float32, jnp.bfloat16
    dma = pltpu.SemaphoreType.DMA
    window = LANES + 2 * RIM

    def local(model, images, footprint, psf_index, exposure_weight, psf_rows, psf_cols):
        rows = model.shape[0]
        blocks = lambda count: pltpu.VMEM((count, rows, LANES), bf16)
        gradient = pl.pallas_call(
            functools.partial(step_kernel, n, strips),
            out_shape=jax.ShapeDtypeStruct(model.shape, f32),
            in_specs=[VMEM, SMEM, SMEM, SMEM, VMEM, VMEM, pl.BlockSpec(memory_space=pl.ANY)],
            out_specs=VMEM,
            scratch_shapes=[
                pltpu.VMEM((rows, n * LANES), bf16),
                blocks(n),
                pltpu.VMEM((n, 2, RIM, LANES), bf16),
                pltpu.VMEM((RANK * LANES, window), bf16),
                pltpu.VMEM((window, RANK * LANES), bf16),
                pltpu.VMEM((RANK * 2 * LANES, 4 * LANES), bf16),
                pltpu.VMEM((4 * LANES, RANK * 2 * LANES), bf16),
                pltpu.VMEM((rows, (n + 2) * LANES), f32),
                pltpu.VMEM((rows, (n + 2) * LANES), bf16),
                blocks(n),
                pltpu.VMEM((n, 2, RIM, LANES), bf16),
                pltpu.VMEM((2 * line, 2, 2, RIM, LANES), bf16),
                blocks(2 * line), blocks(line), blocks(line), blocks(line), blocks(line),
                dma, dma((2, line)), dma((2, line)), dma((2, 2 * line)),
                dma((2, 2)), dma((2, line)), dma((2, line)), dma((2, 2 * line)),
                dma((2, 2 * line)), dma((2, line)), dma((2, line)),
                dma((2, 2 * line, 2, 2)),
            ],
            compiler_params=pltpu.CompilerParams(collective_id=0, has_side_effects=True),
        )(model, footprint.T, psf_index, exposure_weight, psf_rows, psf_cols, images[0])
        return model - step_size * gradient

    placed = (P("strip", "exp"), P("exp", "strip", None), P(), P(), P(), P(), P())
    return jax.shard_map(
        local, mesh=mesh, in_specs=placed, out_specs=P("strip", "exp"), check_vma=False
    )
```

```python
import functools

import jax
import jax.numpy as jnp
from jax import lax
from jax.experimental import pallas as pl
from jax.experimental.pallas import tpu as pltpu
from jax.sharding import PartitionSpec as P

RANK = 4
TAPS = 25
HALF = TAPS // 2
RIM = 16
LANES = 128
step_size = 0.25
MESH = pl.DeviceIdType.MESH
VMEM = pl.BlockSpec(memory_space=pltpu.VMEM)
SMEM = pl.BlockSpec(memory_space=pltpu.SMEM)


def places(n):
    line = n // 4
    if line < 8:
        split = lambda i: (i // 4, (i // 2) % 2, i % 2)
        join = lambda l, p, c: l * 4 + p * 2 + c
    else:
        split = lambda i: ((i // 2) % line, i // (2 * line), i % 2)
        join = lambda l, p, c: p * (2 * line) + l * 2 + c
    return line, split, join


def push(src, dst, send, recv, device):
    copy = pltpu.make_async_remote_copy(
        src_ref=src, dst_ref=dst, send_sem=send, recv_sem=recv, device_id=device,
        device_id_type=MESH,
    )
    copy.start()
    return copy


def greet(devices):
    barrier = pltpu.get_barrier_semaphore()
    for device in devices:
        pl.semaphore_signal(barrier, inc=1, device_id=device, device_id_type=MESH)
    pl.semaphore_wait(barrier, len(devices))


def step_kernel(n, strips, model_ref, footprint, psf_index, weights, psf_rows, psf_cols, image_ref,
                out_ref, image, x, edge, lift, drop, fore, back, pred, res, g, rim, got_rim,
                got_core, to_pair, got_pair, to_line, got_line, image_sem, line_sems, pair_sems,
                core_sems, halo_sems, rim_line_sems, rim_pair_sems,
                rim_core_sems, swap_sems, over_sems, along_sems, rim_sems):
    f32, bf16 = jnp.float32, jnp.bfloat16
    line, split, join = places(n)
    me = lax.axis_index("exp")
    strip = lax.axis_index("strip")
    l, p, c = split(me)
    rows = model_ref.shape[0]
    wide = n * LANES
    parts = rows // LANES
    window = LANES + 2 * RIM
    above, below = (strip + strips - 1) % strips, (strip + 1) % strips
    peers = [{"exp": join((l + q) % line, p, c)} for q in range(line)]
    partner = join(l, p, 1 - c)
    pair = {"exp": join(l, 1 - p, c)}
    core = {"exp": partner}
    aboves = [{"strip": above, "exp": me}, {"strip": above, "exp": partner}]
    belows = [{"strip": below, "exp": me}, {"strip": below, "exp": partner}]

    order = [0]
    for q in range(1, line // 2 + 1):
        order += [q, line - q] if q != line - q else [q]

    fetch = pltpu.make_async_copy(image_ref, image, image_sem)
    fetch.start()
    x[me] = model_ref[...].astype(bf16)
    greet(aboves + belows + [pair, core] + peers[1:])
    along, over, across, edges = {}, {}, {}, {}

    def send_core(at, slot):
        across[at] = push(x.at[slot], x.at[slot], core_sems.at[0, at], core_sems.at[1, at], core)

    def send_core_edge(at, slot):
        edges["core", at] = push(edge.at[slot], edge.at[slot], rim_core_sems.at[0, at],
                                 rim_core_sems.at[1, at], core)

    def send_over(q, slot):
        over[q] = push(x.at[slot], x.at[slot], pair_sems.at[0, q], pair_sems.at[1, q], pair)

    def send_over_edge(q, slot):
        edges["pair", q] = push(edge.at[slot], edge.at[slot], rim_pair_sems.at[0, q],
                                rim_pair_sems.at[1, q], pair)

    def forward_line(q):
        slot = join((l + line - q) % line, p, c)
        along[q].wait_recv()
        send_over(q, slot)
        send_core(q, slot)
        edges["line", q].wait_recv()
        send_over_edge(q, slot)
        send_core_edge(q, slot)

    def forward_pair(q):
        slot = join((l + line - q) % line, 1 - p, c)
        over[q].wait_recv()
        send_core(line + q, slot)
        edges["pair", q].wait_recv()
        send_core_edge(line + q, slot)

    halos = [
        push(x.at[me, pl.ds(rows - RIM, RIM)], edge.at[me, 0], halo_sems.at[0, 0],
             halo_sems.at[1, 0], {"strip": below}),
        push(x.at[me, pl.ds(0, RIM)], edge.at[me, 1], halo_sems.at[0, 1], halo_sems.at[1, 1],
             {"strip": above}),
    ]
    for q in order[1:]:
        along[q] = push(x.at[me], x.at[me], line_sems.at[0, q], line_sems.at[1, q], peers[q])
    send_over(0, me)
    send_core(0, me)

    chosen = psf_index[me]

    def taps_of(table):
        total = jnp.zeros((RANK, TAPS), f32)
        for b in range(table.shape[0]):
            total = total + jnp.where(chosen == b, table[b].astype(f32), 0.0)
        return total.astype(bf16)

    tap = lax.broadcasted_iota(jnp.int32, (TAPS, 384), 0)
    lane = lax.broadcasted_iota(jnp.int32, (TAPS, 384), 1)
    same = (tap == lane).astype(f32).astype(bf16)
    mirror = (tap + lane == TAPS - 1).astype(f32).astype(bf16)
    row_taps = jnp.dot(taps_of(psf_rows), same, preferred_element_type=f32)
    col_taps = taps_of(psf_cols)
    col_fore = jnp.dot(col_taps, mirror, preferred_element_type=f32)
    col_back = jnp.dot(col_taps, same, preferred_element_type=f32)

    def slanted(vector, width, shift):
        spread = jnp.broadcast_to(vector[:, :width], (LANES, width))
        return pltpu.roll(pltpu.roll(spread, 0, 1, stride=1, stride_axis=0), shift, 1)

    none = jnp.zeros((LANES, LANES), bf16)
    for k in range(RANK):
        band = slanted(row_taps[k : k + 1], 256, RIM - HALF)
        lift[k * LANES : (k + 1) * LANES, :] = band[:, :window].astype(bf16)
        band = slanted(col_fore[k : k + 1], 384, LANES - HALF).astype(bf16)
        fore[2 * k * LANES : (2 * k + 1) * LANES, :] = jnp.concatenate([band, none], axis=1)
        fore[(2 * k + 1) * LANES : (2 * k + 2) * LANES, :] = jnp.concatenate([none, band], axis=1)

    for copy in halos:
        copy.wait()
    for q in order[1:]:
        edges["line", q] = push(edge.at[me], edge.at[me], rim_line_sems.at[0, q],
                                rim_line_sems.at[1, q], peers[q])
    send_over_edge(0, me)
    send_core_edge(0, me)

    for k in range(RANK):
        band = slanted(row_taps[k : k + 1], 256, RIM - HALF)
        drop[:, k * LANES : (k + 1) * LANES] = band.T[:window].astype(bf16)
        band = slanted(col_back[k : k + 1], 384, LANES - HALF).astype(bf16)
        for w in range(4):
            for o in range(2):
                d = w - o
                piece = band[:, (2 - d) * LANES : (3 - d) * LANES] if 0 <= d <= 2 else none
                at = (2 * k + o) * LANES
                back[w * LANES : (w + 1) * LANES, at : at + LANES] = piece
    pred[...] = jnp.zeros_like(pred)
    res[:, :LANES] = jnp.zeros((rows, LANES), bf16)
    res[:, wide + LANES :] = jnp.zeros((rows, LANES), bf16)

    top = jnp.where(strip > 0, 1.0, 0.0)
    bottom = jnp.where(strip < strips - 1, 1.0, 0.0)

    def fore_step(at, group, side):
        across[at].wait_recv()
        edges["core", at].wait_recv()
        left = join(group, side, 0)
        right = left + 1
        upper = jnp.concatenate([edge[left, 0], edge[right, 0]], axis=1)
        lower = jnp.concatenate([edge[left, 1], edge[right, 1]], axis=1)
        upper = (upper.astype(f32) * top).astype(bf16)
        lower = (lower.astype(f32) * bottom).astype(bf16)
        middle = jnp.concatenate([x[left], x[right]], axis=1)
        cells = jnp.concatenate([upper, middle, lower], axis=0)
        passes = []
        for s in range(parts):
            out = jnp.dot(lift[...], cells[s * LANES : s * LANES + window],
                          preferred_element_type=f32).astype(bf16)
            passes.append(jnp.concatenate(
                [out[k * LANES : (k + 1) * LANES] for k in range(RANK)], axis=1))
        stack = jnp.concatenate(passes, axis=0)
        at = pl.ds(pl.multiple_of(left * LANES, 2 * LANES), 4 * LANES)
        pred[:, at] = pred[:, at] + jnp.dot(stack, fore[...], preferred_element_type=f32)

    def near_step(q):
        fore_step(q, (l + line - q) % line, p)

    def far_step(q):
        fore_step(line + q, (l + line - q) % line, 1 - p)

    near_step(0)
    forward_pair(0)
    for q in order[1:3]:
        forward_line(q)
    far_step(0)
    for i in range(1, line):
        near_step(order[i])
        forward_pair(order[i])
        if i + 2 < line:
            forward_line(order[i + 2])
        if i >= 2:
            far_step(order[i - 1])
    far_step(order[-1])

    fetch.wait()
    weight = weights[me]
    first_row, last_row = footprint[0, me], footprint[1, me]
    first_col, last_col = footprint[2, me], footprint[3, me]
    row_at = lax.broadcasted_iota(jnp.int32, (rows, 256), 0) + strip * rows
    col_at = lax.broadcasted_iota(jnp.int32, (rows, 256), 1)
    row_ok = (row_at >= first_row) & (row_at < last_row)

    def residual_step(b, carry):
        begin = pl.multiple_of(256 * b, 256)
        inner = pl.ds(pl.multiple_of(256 * b + LANES, LANES), 256)
        inside = row_ok & (col_at >= first_col - begin) & (col_at < last_col - begin)
        value = weight * (pred[:, inner] - image[:, pl.ds(begin, 256)].astype(f32))
        res[:, inner] = jnp.where(inside, value, 0.0).astype(bf16)
        return carry

    lax.fori_loop(0, n // 2, residual_step, 0)

    def back_step(group, side):
        left = join(group, side, 0)
        cells = res[:, pl.ds(pl.multiple_of(left * LANES, 2 * LANES), 4 * LANES)]
        spread = jnp.dot(cells, back[...], preferred_element_type=f32).astype(bf16)
        pieces = []
        for s in range(parts):
            part = spread[s * LANES : (s + 1) * LANES]
            stack = jnp.concatenate(
                [part[:, k * 256 : (k + 1) * 256] for k in range(RANK)], axis=0)
            pieces.append(jnp.dot(drop[...], stack, preferred_element_type=f32))
        joined = [pieces[0][RIM:LANES]]
        for s in range(1, parts):
            joined.append(pieces[s - 1][LANES:] + pieces[s][: 2 * RIM])
            joined.append(pieces[s][2 * RIM : LANES])
        joined.append(pieces[-1][LANES : LANES + RIM])
        total = jnp.concatenate(joined, axis=0).astype(bf16)
        first, last = pieces[0][:RIM].astype(bf16), pieces[-1][LANES + RIM :].astype(bf16)
        for o in range(2):
            cols = slice(o * LANES, (o + 1) * LANES)
            g[left + o] = total[:, cols]
            rim[left + o, 0] = first[:, cols]
            rim[left + o, 1] = last[:, cols]

    swaps, rims, onward, home = {}, {}, {}, {}

    def send_side(q, t):
        group = (l + q) % line
        side = (1 - p, p)[t]
        at = t * line + q
        back_step(group, side)
        swaps[at] = push(g.at[join(group, side, 1 - c)], got_core.at[at],
                         swap_sems.at[0, at], swap_sems.at[1, at], core)
        for cc, whose in ((0, c), (1, 1 - c)):
            slot = join(group, side, whose)
            rims[at, cc, 0] = push(
                rim.at[slot, 0], got_rim.at[at, cc, 0],
                rim_sems.at[0, at, cc, 0], rim_sems.at[1, at, cc, 0], aboves[cc])
            rims[at, cc, 1] = push(
                rim.at[slot, 1], got_rim.at[at, cc, 1],
                rim_sems.at[0, at, cc, 1], rim_sems.at[1, at, cc, 1], belows[cc])

    def chip_sum(at, slot):
        swaps[at].wait_recv()
        for cc in range(2):
            for side in range(2):
                rims[at, cc, side].wait_recv()
        total = g[slot].astype(f32) + got_core[at].astype(f32)
        low = (got_rim[at, 0, 0].astype(f32) + got_rim[at, 1, 0].astype(f32)) * bottom
        high = (got_rim[at, 0, 1].astype(f32) + got_rim[at, 1, 1].astype(f32)) * top
        return jnp.concatenate(
            [total[:RIM] + high, total[RIM : rows - RIM], total[rows - RIM :] + low], axis=0)

    def send_pair(q):
        to_pair[q] = chip_sum(q, join((l + q) % line, 1 - p, c)).astype(bf16)
        onward[q] = push(to_pair.at[q], got_pair.at[q], over_sems.at[0, q], over_sems.at[1, q],
                         pair)

    def send_line(q):
        total = chip_sum(line + q, join((l + q) % line, p, c))
        onward[q].wait_recv()
        total = total + got_pair[q].astype(f32)
        if q:
            to_line[q] = total.astype(bf16)
            home[q] = push(to_line.at[q], got_line.at[q], along_sems.at[0, q],
                           along_sems.at[1, q], peers[q])
        return total

    away = order[::-1]
    for i, q in enumerate(away):
        send_side(q, 0)
        if i:
            send_pair(away[i - 1])
    send_side(away[0], 1)
    send_pair(away[-1])
    for i in range(1, line):
        send_side(away[i], 1)
        send_line(away[i - 1])
    total = send_line(away[-1])
    for q in order[:0:-1]:
        home[q].wait_recv()
        total = total + got_line[q].astype(f32)
    out_ref[...] = total
    for group in (along, over, across, edges, swaps, rims, onward, home):
        for copy in group.values():
            copy.wait_send()


def solution(mesh):
    n, strips = mesh.shape["exp"], mesh.shape["strip"]
    line = n // 4
    f32, bf16 = jnp.float32, jnp.bfloat16
    dma = pltpu.SemaphoreType.DMA
    window = LANES + 2 * RIM

    def local(model, images, footprint, psf_index, exposure_weight, psf_rows, psf_cols):
        rows = model.shape[0]
        blocks = lambda count: pltpu.VMEM((count, rows, LANES), bf16)
        gradient = pl.pallas_call(
            functools.partial(step_kernel, n, strips),
            out_shape=jax.ShapeDtypeStruct(model.shape, f32),
            in_specs=[VMEM, SMEM, SMEM, SMEM, VMEM, VMEM, pl.BlockSpec(memory_space=pl.ANY)],
            out_specs=VMEM,
            scratch_shapes=[
                pltpu.VMEM((rows, n * LANES), bf16),
                blocks(n),
                pltpu.VMEM((n, 2, RIM, LANES), bf16),
                pltpu.VMEM((RANK * LANES, window), bf16),
                pltpu.VMEM((window, RANK * LANES), bf16),
                pltpu.VMEM((RANK * 2 * LANES, 4 * LANES), bf16),
                pltpu.VMEM((4 * LANES, RANK * 2 * LANES), bf16),
                pltpu.VMEM((rows, (n + 2) * LANES), f32),
                pltpu.VMEM((rows, (n + 2) * LANES), bf16),
                blocks(n),
                pltpu.VMEM((n, 2, RIM, LANES), bf16),
                pltpu.VMEM((2 * line, 2, 2, RIM, LANES), bf16),
                blocks(2 * line), blocks(line), blocks(line), blocks(line), blocks(line),
                dma, dma((2, line)), dma((2, line)), dma((2, 2 * line)),
                dma((2, 2)), dma((2, line)), dma((2, line)), dma((2, 2 * line)),
                dma((2, 2 * line)), dma((2, line)), dma((2, line)),
                dma((2, 2 * line, 2, 2)),
            ],
            compiler_params=pltpu.CompilerParams(collective_id=0, has_side_effects=True),
        )(model, footprint.T, psf_index, exposure_weight, psf_rows, psf_cols, images[0])
        return model - step_size * gradient

    placed = (P("strip", "exp"), P("exp", "strip", None), P(), P(), P(), P(), P())
    return jax.shard_map(
        local, mesh=mesh, in_specs=placed, out_specs=P("strip", "exp"), check_vma=False
    )
```
